32 devices in a mesh: state: 4 (over z), basis: 8 (over y, x, core).
Axes of the slice: x: 2, y: 2, z: 4, core: 2. Of those that a mesh axis runs over, the one named last changes fastest.
Arguments:
- states: float32 [8, 64, 64000], P('state', 'basis'), may hold values from -40 to 40
- membrane_step: float32 [40, 40], replicated, may hold values from -1 to 1
- cavity_forward: float32 [64, 64], replicated, may hold values from -0.75 to 0.75
- coupling: float32 [64, 40], replicated, may hold values from 0.25 to 1
- membrane_forward: float32 [40, 40], replicated, may hold values from -1 to 1
- cavity_back: float32 [64, 64], replicated, may hold values from -9 to 9
- membrane_back: float32 [40, 40], replicated, may hold values from -1 to 1
Outputs:
- orthonormal: float32 [8, 64, 64000], P('state', 'basis')
The draws below stay inside these ranges and needn't reach their ends.
All inputs are finite; a program needn't handle non-finite values.
Results may differ from the reference program's by a relative error of at most 0.000075.
Values sent between devices are 32-bit elements; how exact they have to be, the bound alone decides.
A program may use at most 192 MiB of HBM per device.

```python
import math
import jax
import jax.numpy as jnp
from jax import lax

C = 64
M = 40
STATES = 8


def draw_states(key, part):
    key_values, key_scale = jax.random.split(key, 2)
    full_shape = (STATES, C, M * M * M)
    scales = 10.0 ** jax.random.uniform(key_scale, (STATES, 1, 1), jnp.float32)
    independent = jax.random.truncated_normal(key_values, -4.0, 4.0, full_shape, jnp.float32)
    return independent * scales


def draw_cavity_back(key, part):
    key_values, key_scale = jax.random.split(key, 2)
    levels = jnp.arange(C, dtype=jnp.float32)[:, None]
    ramped = jnp.sqrt(1.0 + 2.0 * levels / float(C - 1))
    entries = jax.random.truncated_normal(key_values, -4.0, 4.0, (C, C), jnp.float32)
    exponent = jax.random.uniform(key_scale, (C, 1), jnp.float32)
    return entries * float(C) ** (-0.5) * ramped * 10.0 ** exponent


def normal_values(stream_key, shape, spread, most, kind=jnp.bfloat16):
    return jnp.clip(spread * jax.random.normal(stream_key, shape, jnp.float32), -most, most).astype(kind)


def setup_inputs(seed: int = 0) -> dict:
    key_of = jax.random.split(jax.random.key(seed), 8)
    states = draw_states(jax.random.fold_in(key_of[7], 71), 0)
    membrane_step = normal_values(key_of[1], (M, M), M ** -0.5, 1.0, jnp.float32)
    cavity_forward = normal_values(key_of[2], (C, C), C ** -0.5, 0.75, jnp.float32)
    coupling = jnp.clip(jnp.exp(jax.random.uniform(key_of[3], (C, M), jnp.float32, math.log(0.25), math.log(1.0))), 0.25, 1.0)
    membrane_forward = normal_values(key_of[4], (M, M), M ** -0.5, 1.0, jnp.float32)
    cavity_back = draw_cavity_back(jax.random.fold_in(key_of[7], 71), 0)
    membrane_back = normal_values(key_of[6], (M, M), M ** -0.5, 1.0, jnp.float32)
    return {"states": states, "membrane_step": membrane_step, "cavity_forward": cavity_forward, "coupling": coupling, "membrane_forward": membrane_forward, "cavity_back": cavity_back, "membrane_back": membrane_back}


def propagate_state(state, membrane_step, cavity_forward, coupling, membrane_forward, cavity_back, membrane_back):
    joint = M * M * M
    highest = lax.Precision.HIGHEST
    head = jnp.einsum('ab,cbr->car', membrane_step, state.reshape(C, M, joint // M), precision=highest).reshape(C, joint)
    grid = jnp.dot(cavity_forward, head, precision=highest)
    grid = jnp.einsum('qtk,nk->qtn', grid.reshape(C, joint // M, M), membrane_forward, precision=highest)
    weighted = grid * coupling[:, None, :]
    backward = jnp.einsum('qtn,kn->qtk', weighted, membrane_back, precision=highest).reshape(C, joint)
    return jnp.dot(cavity_back, backward, precision=highest)

def reference(states, membrane_step, cavity_forward, coupling, membrane_forward, cavity_back, membrane_back):
    joint = M * M * M
    highest = lax.Precision.HIGHEST

    def single(state):
        return propagate_state(state, membrane_step, cavity_forward, coupling, membrane_forward, cavity_back, membrane_back)
    propagated = lax.map(single, states)
    flattened = propagated.reshape(STATES, C * joint)
    gram = jnp.dot(flattened, flattened.T, precision=highest) / float(C * joint)
    lower_factor = jnp.linalg.cholesky(gram)
    identity = jnp.eye(STATES, dtype=gram.dtype)
    inverse = lax.linalg.triangular_solve(lower_factor, identity, left_side=True, lower=True)
    orthonormal = jnp.dot(inverse, flattened, precision=highest)
    return orthonormal.reshape(STATES, C, joint)
```

```python
import functools

import jax
import jax.numpy as jnp
from jax import lax
from jax.experimental import pallas as pl
from jax.experimental.pallas import tpu as pltpu
from jax.sharding import PartitionSpec as P

LANES = 128
GROUP_BLOCKS = 16
VMEM_LIMIT = 60 * 1024 * 1024
DIRECT = 2
AHEAD = 1
LAG = 1


def plain_body(
    states, membrane_step, cavity_forward, coupling, membrane_forward, cavity_back, membrane_back
):
    highest = lax.Precision.HIGHEST
    panel_size, level_count, joint = states.shape
    levels_all = cavity_forward.shape[0]
    membrane_levels = membrane_step.shape[0]
    basis_total = float(levels_all * joint)
    head = jnp.einsum(
        "ab,scbr->scar",
        membrane_step,
        states.reshape(panel_size, level_count, membrane_levels, joint // membrane_levels),
        precision=highest,
    )
    head = head.reshape(panel_size, level_count, joint)
    panel_block = lax.all_to_all(head, "basis", split_axis=2, concat_axis=1, tiled=True)
    items, cavity_all, columns = panel_block.shape
    grid = jnp.einsum("qc,kcr->kqr", cavity_forward, panel_block, precision=highest)
    grid = jnp.einsum(
        "kqtm,nm->kqtn",
        grid.reshape(items, cavity_all, columns // membrane_levels, membrane_levels),
        membrane_forward,
        precision=highest,
    )
    weighted = grid * coupling[None, :, None, :]
    backward = jnp.einsum("kqtn,mn->kqtm", weighted, membrane_back, precision=highest)
    backward = backward.reshape(items, cavity_all, columns)
    stepped = jnp.einsum("cq,kqr->kcr", cavity_back, backward, precision=highest)
    spread = lax.all_to_all(stepped, "state", split_axis=2, concat_axis=0, tiled=True)
    state_total, spread_levels, spread_cols = spread.shape
    flattened = spread.reshape(state_total, -1)
    partial_gram = jnp.dot(flattened, flattened.T, precision=highest)
    gram = lax.psum(partial_gram, ("state", "basis")) / basis_total
    lower_factor = jnp.linalg.cholesky(gram)
    identity = jnp.eye(state_total, dtype=gram.dtype)
    inverse = lax.linalg.triangular_solve(lower_factor, identity, left_side=True, lower=True)
    local_result = jnp.dot(inverse, flattened, precision=highest)
    local_result = local_result.reshape(state_total, spread_levels, spread_cols)
    return lax.all_to_all(
        lax.all_to_all(local_result, "state", split_axis=0, concat_axis=2, tiled=True),
        "basis",
        split_axis=1,
        concat_axis=2,
        tiled=True,
    )


def split2(x):
    hi = x.astype(jnp.bfloat16)
    lo = (x - hi.astype(jnp.float32)).astype(jnp.bfloat16)
    return hi, lo


def bdot(a, b):
    return jnp.dot(a, b, preferred_element_type=jnp.float32)


def left3(wh, wl, x):
    xh, xl = split2(x)
    return bdot(jnp.concatenate([wh, wl, wh], axis=1), jnp.concatenate([xh, xh, xl], axis=0))


def right3(x, wh, wl):
    xh, xl = split2(x)
    return bdot(xh, wh) + bdot(xl, wh) + bdot(xh, wl)


def kron_left(w, reps, out_ref_h, out_ref_l):
    m = w.shape[0]
    n = m * reps
    row = lax.broadcasted_iota(jnp.int32, (n, m), 0)
    col = lax.broadcasted_iota(jnp.int32, (n, m), 1)
    left = (row // reps == col).astype(jnp.bfloat16)
    right_row = lax.broadcasted_iota(jnp.int32, (m, n), 0)
    right_col = lax.broadcasted_iota(jnp.int32, (m, n), 1)
    right = (right_col // reps == right_row).astype(jnp.bfloat16)
    a = lax.broadcasted_iota(jnp.int32, (n, 1), 0)
    b = lax.broadcasted_iota(jnp.int32, (1, n), 1)
    keep = lax.rem(a, reps) == lax.rem(b, reps)
    for part, ref in zip(split2(w), (out_ref_h, out_ref_l)):
        full = bdot(bdot(left, part).astype(jnp.bfloat16), right)
        ref[...] = jnp.where(keep, full, 0.0).astype(jnp.bfloat16)


def kron_lanes(w_t, reps, out_ref_h, out_ref_l):
    m = w_t.shape[0]
    n = m * reps
    left = (
        lax.rem(lax.broadcasted_iota(jnp.int32, (n, m), 0), m)
        == lax.broadcasted_iota(jnp.int32, (n, m), 1)
    ).astype(jnp.bfloat16)
    right = (
        lax.rem(lax.broadcasted_iota(jnp.int32, (m, n), 1), m)
        == lax.broadcasted_iota(jnp.int32, (m, n), 0)
    ).astype(jnp.bfloat16)
    a = lax.broadcasted_iota(jnp.int32, (n, 1), 0)
    b = lax.broadcasted_iota(jnp.int32, (1, n), 1)
    keep = a // m == b // m
    for part, ref in zip(split2(w_t), (out_ref_h, out_ref_l)):
        full = bdot(bdot(left, part).astype(jnp.bfloat16), right)
        ref[...] = jnp.where(keep, full, 0.0).astype(jnp.bfloat16)


def remote(src, dst, send_sem, recv_sem, axis, peer):
    return pltpu.make_async_remote_copy(
        src_ref=src,
        dst_ref=dst,
        send_sem=send_sem,
        recv_sem=recv_sem,
        device_id={axis: peer},
        device_id_type=pl.DeviceIdType.MESH,
    )


def peers_of(axis, size):
    me = lax.axis_index(axis)
    return me, [lax.rem(me + d, size) for d in range(1, size)]


def lane_groups(cols, group):
    out = []
    for at in range(0, cols, group):
        n = min(group, cols - at)
        out.append((at, n, -(-n // LANES) * LANES))
    return out


def tiles_of(at, n, ns):
    for t in range(n // LANES):
        yield [ns * at + s * (n // LANES) * LANES + t * LANES for s in range(ns)]
    if n % LANES:
        yield [ns * at + ns * (n // LANES) * LANES]


def load_pair(ref, low, offs):
    vals = [ref[:, at : at + LANES] for at in offs]
    if len(vals) == 1:
        v = vals[0]
        vals = [jnp.where(low, v, 0.0), jnp.where(low, pltpu.roll(v, LANES // 2, 1), 0.0)]
    return vals


def store_pair(ref, low, offs, vals):
    if len(offs) == 1:
        vals = [jnp.where(low, vals[0], pltpu.roll(vals[1], LANES // 2, 1))]
    for at, v in zip(offs, vals):
        ref[:, at : at + LANES] = v


def step_kernel(
    nz,
    nb,
    x_ref,
    ms_ref,
    fc_ref,
    cp_ref,
    fk_ref,
    bc_ref,
    bk_ref,
    o_ref,
    xin,
    kh,
    kl,
    xs,
    outgo,
    fh,
    fl,
    bh,
    bl,
    cps,
    block,
    panels,
    gacc,
    gram_b,
    gram_z,
    splat,
    mixed,
    sums,
    home,
    in_sem,
    b_send,
    b_recv,
    z_send,
    z_recv,
    gb_send,
    gb_recv,
    gz_send,
    gz_recv,
    c_send,
    c_recv,
):
    ns, lev, _ = xin.shape
    nq = block.shape[0]
    rows = nb // 2
    total = nz * ns
    c_all = fc_ref.shape[0]
    m = fk_ref.shape[0]
    cols = x_ref.shape[2] // m
    group = m * GROUP_BLOCKS
    groups = lane_groups(cols, group)
    ng = len(groups)
    padded = [pl.ds(ns * at, ns * wide) for at, _, wide in groups]
    packed = [pl.ds(ns * at, ns * n) for at, n, _ in groups]
    me_b, others_b = peers_of("basis", nb)
    me_z, others_z = peers_of("state", nz)
    parity = lax.rem(me_b, 2)
    inner = (me_z == 1) | (me_z == 2)
    low = lax.broadcasted_iota(jnp.int32, (lev, LANES), 1) < LANES // 2

    def to_basis(q, g, peer):
        return remote(
            outgo.at[peer, q, :, padded[g]],
            block.at[q, me_b, :, padded[g]],
            b_send.at[q, g, peer],
            b_recv.at[q, g, me_b],
            "basis",
            peer,
        )

    def from_basis(q, g, peer):
        return remote(
            outgo.at[me_b, q, :, padded[g]],
            block.at[q, peer, :, padded[g]],
            b_send.at[q, g, peer],
            b_recv.at[q, g, peer],
            "basis",
            peer,
        )

    def along(src, slot, q, h, g, peer):
        return remote(
            src.at[q, h, :, :, packed[g]],
            panels.at[slot, q, h, :, :, packed[g]],
            z_send.at[slot, q, h, g],
            z_recv.at[slot, q, h, g],
            "state",
            peer,
        )

    def push(k, q, h, g, peer):
        along(panels.at[k], k, q, h, g, peer).start()

    def arrived(slot, q, h, g):
        along(mixed, slot, q, h, g, others_z[0]).wait_recv()

    def sent(slot, q, h, g):
        along(mixed, slot, q, h, g, others_z[0]).wait_send()

    def home_out(q, h, g, r):
        peer = 2 * r + h
        return remote(
            mixed.at[q, h, r, :, packed[g]],
            home.at[q, me_b, :, packed[g]],
            c_send.at[q, g, peer],
            c_recv.at[q, g, me_b],
            "basis",
            peer,
        )

    def home_in(q, g, peer):
        return remote(
            mixed.at[q, 0, 0, :, packed[g]],
            home.at[q, peer, :, packed[g]],
            c_send.at[q, g, peer],
            c_recv.at[q, g, peer],
            "basis",
            peer,
        )

    barrier = pltpu.get_barrier_semaphore()
    for axis, others in (("basis", others_b), ("state", others_z)):
        for peer in others:
            pl.semaphore_signal(
                barrier, inc=1, device_id={axis: peer}, device_id_type=pl.DeviceIdType.MESH
            )
    loads = [pltpu.make_async_copy(x_ref.at[s], xin.at[s], in_sem.at[s]) for s in range(ns)]
    for load in loads:
        load.start()
    kron_left(ms_ref[...], lev, kh, kl)
    gacc[...] = jnp.zeros_like(gacc)
    for load in loads:
        load.wait()
    for g, (at, n, wide) in enumerate(groups):
        for i in range(m):
            for s in range(ns):
                xs[i * lev : (i + 1) * lev, s * wide : s * wide + n] = xin[
                    s, :, i * cols + at : i * cols + at + n
                ]
        xh, xl = split2(xs[:, : ns * wide])
        y = bdot(kh[...], xh) + bdot(kl[...], xh) + bdot(kh[...], xl)
        outgo[:, :, :, padded[g]] = y.reshape(nb, nq, lev, ns * wide)
        if g == 0:
            pl.semaphore_wait(barrier, nb + nz - 2)
        for peer in others_b:
            to_basis(0, g, peer).start()
        if g == 0:
            kron_lanes(fk_ref[...].T, GROUP_BLOCKS, fh, fl)
            kron_lanes(bk_ref[...].T, GROUP_BLOCKS, bh, bl)
            tile_m = (
                lax.rem(lax.broadcasted_iota(jnp.int32, (m, group), 1), m)
                == lax.broadcasted_iota(jnp.int32, (m, group), 0)
            ).astype(jnp.float32)
            factor = jnp.dot(cp_ref[...].T, tile_m, precision=lax.Precision.HIGHEST)
            for s in range(ns):
                cps[s * c_all : (s + 1) * c_all] = factor

    @pl.loop(1, nq)
    def _(q):
        for g in range(ng):
            for peer in others_b:
                to_basis(q, g, peer).start()

    ch, cl = split2(fc_ref[...])
    dh, dl = split2(bc_ref[...])
    far, relay_half, gram_half = 3 * (me_z - 1), me_z - 1, 2 - me_z

    def relay(q):
        for g in range(ng):
            arrived(far, q, relay_half, g)
            push(far, q, relay_half, g, 3 - me_z)

    @pl.loop(0, nq)
    def _(q):
        for g, (at, n, wide) in enumerate(groups):
            block[q, me_b, :, padded[g]] = outgo[me_b, q, :, padded[g]]
            for peer in others_b:
                from_basis(q, g, peer).wait_recv()
            y = left3(ch, cl, block[q, :, :, padded[g]].reshape(c_all, ns * wide))
            y = jnp.concatenate([y[:, s * wide : (s + 1) * wide] for s in range(ns)], axis=0)
            y = right3(y, fh[:wide, :wide], fl[:wide, :wide]) * cps[:, :wide]
            y = right3(y, bh[:wide, :wide], bl[:wide, :wide])
            y = jnp.concatenate([y[s * c_all : (s + 1) * c_all] for s in range(ns)], axis=1)
            y = left3(dh, dl, y)
            if n % LANES:
                full = n - n % LANES
                edge = [y[:, s * wide + full : s * wide + full + LANES] for s in range(ns)]
                wide_low = lax.broadcasted_iota(jnp.int32, edge[0].shape, 1) < LANES // 2
                edge = jnp.where(wide_low, edge[0], pltpu.roll(edge[1], LANES // 2, 1))
                y = jnp.concatenate(
                    [y[:, s * wide : s * wide + full] for s in range(ns)] + [edge], axis=1
                )
            y = y.reshape(rows, 2, lev, ns * n)
            for h in range(2):
                panels[me_z, q, h, :, :, packed[g]] = y[:, h]

            @pl.when(me_z == 0)
            def _():
                push(0, q, 0, g, 1)
                push(0, q, 1, g, 1)

            @pl.when(me_z == 1)
            def _():
                push(1, q, 0, g, 2)

            @pl.when(me_z == 2)
            def _():
                push(2, q, 1, g, 1)

                @pl.when(q < DIRECT)
                def _():
                    push(2, q, 0, g, 3)

            @pl.when(me_z == 3)
            def _():
                push(3, q, 1, g, 2)
                push(3, q, 0, g, 2)

        @pl.when(inner & (q >= 1) & (q <= 2))
        def _():
            relay(q - 1)

    pairs = [(a, b) for a in range(total) for b in range(a + 1)]

    def second(q, g):
        push(1, q, 1, g, 2)
        push(0, q, 1, g, 2)

    def gram_piece(q, h):
        def body(r, accs):
            accs = list(accs)
            for at, n, _ in groups:
                for offs in tiles_of(at, n, ns):
                    vals = []
                    for k in range(nz):
                        vals += load_pair(panels.at[k, q, h, r], low, offs)
                    for p, (a, b) in enumerate(pairs):
                        accs[p] = accs[p] + vals[a] * vals[b]
            return tuple(accs)

        zero = jnp.zeros((lev, LANES), jnp.float32)
        for p, acc in enumerate(lax.fori_loop(0, rows, body, (zero,) * len(pairs))):
            gacc[p] += acc

    row = lax.broadcasted_iota(jnp.int32, (total, LANES), 0)
    col = lax.broadcasted_iota(jnp.int32, (total, LANES), 1)

    @pl.when(inner)
    def _():
        relay(2)

        @pl.loop(0, nq)
        def _(q):
            @pl.when(q == 2)
            def _():
                relay(3)

            @pl.when(q == 3)
            def _():
                relay(4)

                @pl.when(me_z == 1)
                def _():
                    for g in range(AHEAD):
                        second(0, g)

            for g in range(ng):
                arrived(0, q, gram_half, g)
                arrived(3, q, gram_half, g)
                arrived(3 - me_z, q, gram_half, g)

            @pl.when((me_z == 2) & (q < DIRECT))
            def _():
                for g in range(ng):
                    push(1, q, 0, g, 3)
                    push(0, q, 0, g, 3)

            gram_piece(q, gram_half)

        partial = jnp.zeros((total, LANES), jnp.float32)
        for p, (a, b) in enumerate(pairs):
            v = jnp.sum(jnp.sum(gacc[p], axis=0, keepdims=True), axis=1, keepdims=True)
            here = ((row == a) & (col == b)) | ((row == b) & (col == a))
            partial = jnp.where(here, v, partial)
        gram_b[me_b] = partial
        for peer in others_b:
            remote(
                gram_b.at[me_b],
                gram_b.at[me_b],
                gb_send.at[peer],
                gb_recv.at[me_b],
                "basis",
                peer,
            ).start()
        for peer in others_b:
            remote(
                gram_b.at[me_b],
                gram_b.at[peer],
                gb_send.at[peer],
                gb_recv.at[peer],
                "basis",
                peer,
            ).wait()
        partial = gram_b[0]
        for i in range(1, nb):
            partial = partial + gram_b[i]
        gram_z[me_z] = partial
        for peer in others_z:
            remote(
                gram_z.at[me_z],
                gram_z.at[me_z],
                gz_send.at[peer],
                gz_recv.at[me_z],
                "state",
                peer,
            ).start()

        @pl.when(me_z == 1)
        def _():
            for g in range(AHEAD, ng):
                second(0, g)

            @pl.loop(1, nq)
            def _(q):
                for g in range(ng):
                    second(q, g)

    for source in (1, 2):
        @pl.when(me_z != source)
        def _():
            remote(
                gram_z.at[source],
                gram_z.at[source],
                gz_send.at[source],
                gz_recv.at[source],
                "state",
                others_z[0],
            ).wait_recv()

    gram = (gram_z[1] + gram_z[2]) / float(c_all * m * cols)
    pair = jnp.where(col == row + total, 1.0, gram)
    diag = jnp.ones((total, 1), jnp.float32)
    for j in range(total):
        pivot = pair[j : j + 1, j : j + 1]
        diag = jnp.where(row[:, :1] == j, pivot, diag)
        if j < total - 1:
            factor = jnp.where(row[:, :1] > j, pair[:, j : j + 1] / pivot, 0.0)
            pair = pair - factor * pair[j : j + 1, :]
    pair = pair / jnp.sqrt(diag)
    for b in range(total):
        for a in range(b + 1):
            splat[b * total + a] = jnp.broadcast_to(
                pair[b : b + 1, total + a : total + a + 1], (lev, LANES)
            )

    def mix(q, h, g, ins, outs):
        at, n, _ = groups[g]

        @pl.loop(0, rows)
        def _(r):
            for offs in tiles_of(at, n, ns):
                vals = {k: load_pair(panels.at[k, q, h, r], low, offs) for k, _ in ins}
                for panel, dst in outs:
                    res = []
                    for s in range(ns):
                        b = panel * ns + s
                        acc = None
                        for k, ready in ins:
                            if ready:
                                terms = [vals[k][s]]
                            else:
                                terms = [
                                    splat[b * total + k * ns + a] * vals[k][a]
                                    for a in range(ns)
                                    if k * ns + a <= b
                                ]
                            for term in terms:
                                acc = term if acc is None else acc + term
                        res.append(acc)
                    store_pair(dst.at[q, h, r], low, offs, res)

    def plain(*ks):
        return [(k, False) for k in ks]

    def send_home(q, h, g):
        for r in range(rows):
            mine = 2 * r + h == me_b

            @pl.when(jnp.logical_not(mine))
            def _():
                home_out(q, h, g, r).start()

            @pl.when(mine)
            def _():
                home[q, me_b, :, packed[g]] = mixed[q, h, r, :, packed[g]]

    @pl.loop(0, nq)
    def _(q):
        for g in range(ng):
            @pl.when(me_z == 0)
            def _():
                for h in range(2):
                    mix(q, h, g, plain(0), [(0, mixed)])

            @pl.when(me_z == 1)
            def _():
                for h in range(2):
                    mix(q, h, g, plain(0, 1), [(1, mixed)])

            @pl.when(me_z == 2)
            def _():
                mix(q, 0, g, plain(0, 1, 2), [(2, mixed), (3, sums)])

                @pl.when(q >= DIRECT)
                def _():
                    along(sums, 0, q, 0, g, 3).start()

            @pl.when(me_z == 3)
            def _():
                arrived(0, q, 0, g)

                @pl.when(q < DIRECT)
                def _():
                    arrived(1, q, 0, g)
                    arrived(2, q, 0, g)
                    mix(q, 0, g, plain(0, 1, 2, 3), [(3, mixed)])

                @pl.when(q >= DIRECT)
                def _():
                    mix(q, 0, g, [(0, True), (3, False)], [(3, mixed)])

            send_home(q, 0, g)

            @pl.when(me_z <= 1)
            def _():
                send_home(q, 1, g)

    def place(q, g):
        at, n, _ = groups[g]
        full = n - n % LANES
        for peer in others_b:
            home_in(q, g, peer).wait_recv()
        for b in range(nb):
            lane = (b * nq + q) * cols + at
            for s in range(ns):
                src = ns * at + s * full
                o_ref[s, :, lane : lane + full] = home[q, b, :, src : src + full]
                if n % LANES:
                    src = ns * at + ns * full + s * (n - full)
                    o_ref[s, :, lane + full : lane + n] = home[q, b, :, src : src + n - full]

    order = [(q, g) for q in range(nq) for g in range(ng)]
    for k, (q, g) in enumerate(order):
        @pl.when(me_z == 2)
        def _():
            arrived(0, q, 1, g)
            arrived(1, q, 1, g)
            mix(q, 1, g, plain(0, 1, 2), [(2, mixed), (3, sums)])
            along(sums, 0, q, 1, g, 3).start()

        @pl.when(me_z == 3)
        def _():
            arrived(0, q, 1, g)
            mix(q, 1, g, [(0, True), (3, False)], [(3, mixed)])

        @pl.when(me_z >= 2)
        def _():
            send_home(q, 1, g)

        if k >= LAG:
            place(*order[k - LAG])
    for k in range(len(order) - LAG, len(order)):
        place(*order[k])

    @pl.loop(0, nq)
    def _(q):
        for g in range(ng):
            for peer in others_b:
                to_basis(q, g, peer).wait_send()
                home_in(q, g, peer).wait_send()

            @pl.when(me_z == 0)
            def _():
                for h in range(2):
                    sent(0, q, h, g)

            @pl.when(me_z == 1)
            def _():
                for k in range(2):
                    for h in range(2):
                        sent(k, q, h, g)

            @pl.when(me_z == 2)
            def _():
                sent(2, q, 1, g)
                sent(3, q, 1, g)
                sent(0, q, 0, g)
                sent(0, q, 1, g)

                @pl.when(q < DIRECT)
                def _():
                    sent(1, q, 0, g)
                    sent(2, q, 0, g)

            @pl.when(me_z == 3)
            def _():
                for h in range(2):
                    sent(3, q, h, g)

    @pl.when(inner)
    def _():
        for peer in others_z:
            remote(
                gram_z.at[me_z],
                gram_z.at[me_z],
                gz_send.at[peer],
                gz_recv.at[me_z],
                "state",
                peer,
            ).wait_send()


def fast_body(
    nz,
    nb,
    states,
    membrane_step,
    cavity_forward,
    coupling,
    membrane_forward,
    cavity_back,
    membrane_back,
):
    f32, bf16 = jnp.float32, jnp.bfloat16
    ns, lev, joint = states.shape
    m = membrane_step.shape[0]
    c_all = cavity_forward.shape[0]
    nq, rows = m // nb, nb // 2
    cols = joint // m
    group = m * GROUP_BLOCKS
    groups = lane_groups(cols, group)
    ng = len(groups)
    width = sum(wide for _, _, wide in groups)
    total = nz * ns
    dma = pltpu.SemaphoreType.DMA
    vmem = pl.BlockSpec(memory_space=pltpu.VMEM)
    panel = (nq, 2, rows, lev, ns * cols)
    return pl.pallas_call(
        functools.partial(step_kernel, nz, nb),
        in_specs=[pl.BlockSpec(memory_space=pl.ANY)] + [vmem] * 6,
        out_specs=vmem,
        out_shape=jax.ShapeDtypeStruct((ns, lev, joint), f32),
        scratch_shapes=[
            pltpu.VMEM((ns, lev, joint), f32),
            pltpu.VMEM((m * lev, m * lev), bf16),
            pltpu.VMEM((m * lev, m * lev), bf16),
            pltpu.VMEM((m * lev, ns * group), f32),
            pltpu.VMEM((nb, nq, lev, ns * width), f32),
        ]
        + [pltpu.VMEM((group, group), bf16)] * 4
        + [
            pltpu.VMEM((ns * c_all, group), f32),
            pltpu.VMEM((nq, nb, lev, ns * width), f32),
            pltpu.VMEM((nz,) + panel, f32),
            pltpu.VMEM((total * (total + 1) // 2, lev, LANES), f32),
            pltpu.VMEM((nb, total, LANES), f32),
            pltpu.VMEM((nz, total, LANES), f32),
            pltpu.VMEM((total * total, lev, LANES), f32),
            pltpu.VMEM(panel, f32),
            pltpu.VMEM(panel, f32),
            pltpu.VMEM((nq, nb, lev, ns * cols), f32),
            dma((ns,)),
        ]
        + [dma((nq, ng, nb))] * 2
        + [dma((nz, nq, 2, ng))] * 2
        + [dma((nb,))] * 2
        + [dma((nz,))] * 2
        + [dma((nq, ng, nb))] * 2,
        compiler_params=pltpu.CompilerParams(
            vmem_limit_bytes=VMEM_LIMIT, collective_id=0, has_side_effects=True
        ),
    )(
        states,
        membrane_step,
        cavity_forward,
        coupling.T,
        membrane_forward,
        cavity_back,
        membrane_back,
    )


def solution(mesh):
    nz, nb = mesh.shape["state"], mesh.shape["basis"]
    in_specs = (P("state", "basis", None), P(), P(), P(), P(), P(), P())
    out_specs = P("state", "basis", None)

    def body(states, membrane_step, cavity_forward, *rest):
        m, c_all = membrane_step.shape[0], cavity_forward.shape[0]
        divides = nz == 4 and m == 5 * nb and nb % 2 == 0
        packs = states.shape[0] == 2 and m * m % LANES == LANES // 2
        if divides and packs and states.shape[1] == 8 and c_all == 8 * nb:
            return fast_body(nz, nb, states, membrane_step, cavity_forward, *rest)
        return plain_body(states, membrane_step, cavity_forward, *rest)

    return jax.shard_map(body, mesh=mesh, in_specs=in_specs, out_specs=out_specs, check_vma=False)
```

```python
import functools

import jax
import jax.numpy as jnp
from jax import lax
from jax.experimental import pallas as pl
from jax.experimental.pallas import tpu as pltpu
from jax.sharding import PartitionSpec as P

LANES = 128
GROUP_BLOCKS = 16
VMEM_LIMIT = 60 * 1024 * 1024
DIRECT = 2
AHEAD = 3
LAG = 1


def plain_body(
    states, membrane_step, cavity_forward, coupling, membrane_forward, cavity_back, membrane_back
):
    highest = lax.Precision.HIGHEST
    panel_size, level_count, joint = states.shape
    levels_all = cavity_forward.shape[0]
    membrane_levels = membrane_step.shape[0]
    basis_total = float(levels_all * joint)
    head = jnp.einsum(
        "ab,scbr->scar",
        membrane_step,
        states.reshape(panel_size, level_count, membrane_levels, joint // membrane_levels),
        precision=highest,
    )
    head = head.reshape(panel_size, level_count, joint)
    panel_block = lax.all_to_all(head, "basis", split_axis=2, concat_axis=1, tiled=True)
    items, cavity_all, columns = panel_block.shape
    grid = jnp.einsum("qc,kcr->kqr", cavity_forward, panel_block, precision=highest)
    grid = jnp.einsum(
        "kqtm,nm->kqtn",
        grid.reshape(items, cavity_all, columns // membrane_levels, membrane_levels),
        membrane_forward,
        precision=highest,
    )
    weighted = grid * coupling[None, :, None, :]
    backward = jnp.einsum("kqtn,mn->kqtm", weighted, membrane_back, precision=highest)
    backward = backward.reshape(items, cavity_all, columns)
    stepped = jnp.einsum("cq,kqr->kcr", cavity_back, backward, precision=highest)
    spread = lax.all_to_all(stepped, "state", split_axis=2, concat_axis=0, tiled=True)
    state_total, spread_levels, spread_cols = spread.shape
    flattened = spread.reshape(state_total, -1)
    partial_gram = jnp.dot(flattened, flattened.T, precision=highest)
    gram = lax.psum(partial_gram, ("state", "basis")) / basis_total
    lower_factor = jnp.linalg.cholesky(gram)
    identity = jnp.eye(state_total, dtype=gram.dtype)
    inverse = lax.linalg.triangular_solve(lower_factor, identity, left_side=True, lower=True)
    local_result = jnp.dot(inverse, flattened, precision=highest)
    local_result = local_result.reshape(state_total, spread_levels, spread_cols)
    return lax.all_to_all(
        lax.all_to_all(local_result, "state", split_axis=0, concat_axis=2, tiled=True),
        "basis",
        split_axis=1,
        concat_axis=2,
        tiled=True,
    )


def split2(x):
    hi = x.astype(jnp.bfloat16)
    lo = (x - hi.astype(jnp.float32)).astype(jnp.bfloat16)
    return hi, lo


def bdot(a, b):
    return jnp.dot(a, b, preferred_element_type=jnp.float32)


def left3(wh, wl, x):
    xh, xl = split2(x)
    return bdot(jnp.concatenate([wh, wl, wh], axis=1), jnp.concatenate([xh, xh, xl], axis=0))


def right3(x, wh, wl):
    xh, xl = split2(x)
    return bdot(xh, wh) + bdot(xl, wh) + bdot(xh, wl)


def kron_left(w, reps, out_ref_h, out_ref_l):
    m = w.shape[0]
    n = m * reps
    row = lax.broadcasted_iota(jnp.int32, (n, m), 0)
    col = lax.broadcasted_iota(jnp.int32, (n, m), 1)
    left = (row // reps == col).astype(jnp.bfloat16)
    right_row = lax.broadcasted_iota(jnp.int32, (m, n), 0)
    right_col = lax.broadcasted_iota(jnp.int32, (m, n), 1)
    right = (right_col // reps == right_row).astype(jnp.bfloat16)
    a = lax.broadcasted_iota(jnp.int32, (n, 1), 0)
    b = lax.broadcasted_iota(jnp.int32, (1, n), 1)
    keep = lax.rem(a, reps) == lax.rem(b, reps)
    for part, ref in zip(split2(w), (out_ref_h, out_ref_l)):
        full = bdot(bdot(left, part).astype(jnp.bfloat16), right)
        ref[...] = jnp.where(keep, full, 0.0).astype(jnp.bfloat16)


def kron_lanes(w_t, reps, out_ref_h, out_ref_l):
    m = w_t.shape[0]
    n = m * reps
    left = (
        lax.rem(lax.broadcasted_iota(jnp.int32, (n, m), 0), m)
        == lax.broadcasted_iota(jnp.int32, (n, m), 1)
    ).astype(jnp.bfloat16)
    right = (
        lax.rem(lax.broadcasted_iota(jnp.int32, (m, n), 1), m)
        == lax.broadcasted_iota(jnp.int32, (m, n), 0)
    ).astype(jnp.bfloat16)
    a = lax.broadcasted_iota(jnp.int32, (n, 1), 0)
    b = lax.broadcasted_iota(jnp.int32, (1, n), 1)
    keep = a // m == b // m
    for part, ref in zip(split2(w_t), (out_ref_h, out_ref_l)):
        full = bdot(bdot(left, part).astype(jnp.bfloat16), right)
        ref[...] = jnp.where(keep, full, 0.0).astype(jnp.bfloat16)


def remote(src, dst, send_sem, recv_sem, axis, peer):
    return pltpu.make_async_remote_copy(
        src_ref=src,
        dst_ref=dst,
        send_sem=send_sem,
        recv_sem=recv_sem,
        device_id={axis: peer},
        device_id_type=pl.DeviceIdType.MESH,
    )


def peers_of(axis, size):
    me = lax.axis_index(axis)
    return me, [lax.rem(me + d, size) for d in range(1, size)]


def lane_groups(cols, group):
    out = []
    for at in range(0, cols, group):
        n = min(group, cols - at)
        out.append((at, n, -(-n // LANES) * LANES))
    return out


def tiles_of(at, n, ns):
    for t in range(n // LANES):
        yield [ns * at + s * (n // LANES) * LANES + t * LANES for s in range(ns)]
    if n % LANES:
        yield [ns * at + ns * (n // LANES) * LANES]


def load_pair(ref, low, offs):
    vals = [ref[:, at : at + LANES] for at in offs]
    if len(vals) == 1:
        v = vals[0]
        vals = [jnp.where(low, v, 0.0), jnp.where(low, pltpu.roll(v, LANES // 2, 1), 0.0)]
    return vals


def store_pair(ref, low, offs, vals):
    if len(offs) == 1:
        vals = [jnp.where(low, vals[0], pltpu.roll(vals[1], LANES // 2, 1))]
    for at, v in zip(offs, vals):
        ref[:, at : at + LANES] = v


def step_kernel(
    nz,
    nb,
    x_ref,
    ms_ref,
    fc_ref,
    cp_ref,
    fk_ref,
    bc_ref,
    bk_ref,
    o_ref,
    xin,
    kh,
    kl,
    kcat,
    xs,
    outgo,
    fh,
    fl,
    bh,
    bl,
    cps,
    block,
    panels,
    gacc,
    gram_b,
    gram_z,
    splat,
    mixed,
    sums,
    home,
    in_sem,
    b_send,
    b_recv,
    z_send,
    z_recv,
    gb_send,
    gb_recv,
    gz_send,
    gz_recv,
    c_send,
    c_recv,
):
    ns, lev, _ = xin.shape
    nq = block.shape[0]
    rows = nb // 2
    total = nz * ns
    c_all = fc_ref.shape[0]
    m = fk_ref.shape[0]
    cols = x_ref.shape[2] // m
    group = m * GROUP_BLOCKS
    groups = lane_groups(cols, group)
    ng = len(groups)
    padded = [pl.ds(ns * at, ns * wide) for at, _, wide in groups]
    packed = [pl.ds(ns * at, ns * n) for at, n, _ in groups]
    me_b, others_b = peers_of("basis", nb)
    me_z, others_z = peers_of("state", nz)
    parity = lax.rem(me_b, 2)
    inner = (me_z == 1) | (me_z == 2)
    low = lax.broadcasted_iota(jnp.int32, (lev, LANES), 1) < LANES // 2

    def to_basis(q, g, peer):
        return remote(
            outgo.at[peer, q, :, padded[g]],
            block.at[q, me_b, :, padded[g]],
            b_send.at[q, g, peer],
            b_recv.at[q, g, me_b],
            "basis",
            peer,
        )

    def from_basis(q, g, peer):
        return remote(
            outgo.at[me_b, q, :, padded[g]],
            block.at[q, peer, :, padded[g]],
            b_send.at[q, g, peer],
            b_recv.at[q, g, peer],
            "basis",
            peer,
        )

    def along(src, slot, q, h, g, peer):
        return remote(
            src.at[q, h, :, :, packed[g]],
            panels.at[slot, q, h, :, :, packed[g]],
            z_send.at[slot, q, h, g],
            z_recv.at[slot, q, h, g],
            "state",
            peer,
        )

    def push(k, q, h, g, peer):
        along(panels.at[k], k, q, h, g, peer).start()

    def arrived(slot, q, h, g):
        along(mixed, slot, q, h, g, others_z[0]).wait_recv()

    def sent(slot, q, h, g):
        along(mixed, slot, q, h, g, others_z[0]).wait_send()

    def home_out(q, h, g, r):
        peer = 2 * r + h
        return remote(
            mixed.at[q, h, r, :, packed[g]],
            home.at[q, me_b, :, packed[g]],
            c_send.at[q, g, peer],
            c_recv.at[q, g, me_b],
            "basis",
            peer,
        )

    def home_in(q, g, peer):
        return remote(
            mixed.at[q, 0, 0, :, packed[g]],
            home.at[q, peer, :, packed[g]],
            c_send.at[q, g, peer],
            c_recv.at[q, g, peer],
            "basis",
            peer,
        )

    barrier = pltpu.get_barrier_semaphore()
    for axis, others in (("basis", others_b), ("state", others_z)):
        for peer in others:
            pl.semaphore_signal(
                barrier, inc=1, device_id={axis: peer}, device_id_type=pl.DeviceIdType.MESH
            )
    def load(s, c):
        lanes = pl.ds(c * nb * cols, nb * cols)
        return pltpu.make_async_copy(x_ref.at[s, :, lanes], xin.at[s, :, lanes], in_sem.at[s, c])

    for c in range(m // nb):
        for s in range(ns):
            load(s, c).start()
    kron_left(ms_ref[...], lev, kh, kl)
    kcat[...] = jnp.concatenate([kh[...], kl[...], kh[...]], axis=1)
    for g, (at, n, wide) in enumerate(groups):
        for i in range(m):
            for s in range(ns):
                if g == 0 and i % nb == 0:
                    load(s, i // nb).wait()
                xs[i * lev : (i + 1) * lev, s * wide : s * wide + n] = xin[
                    s, :, i * cols + at : i * cols + at + n
                ]
        xh, xl = split2(xs[:, : ns * wide])
        y = bdot(kcat[...], jnp.concatenate([xh, xh, xl], axis=0))
        outgo[:, :, :, padded[g]] = y.reshape(nb, nq, lev, ns * wide)
        if g == 0:
            pl.semaphore_wait(barrier, nb + nz - 2)
        for peer in others_b:
            to_basis(0, g, peer).start()
        if g == 0:
            kron_lanes(fk_ref[...].T, GROUP_BLOCKS, fh, fl)
            kron_lanes(bk_ref[...].T, GROUP_BLOCKS, bh, bl)
            tile_m = (
                lax.rem(lax.broadcasted_iota(jnp.int32, (m, group), 1), m)
                == lax.broadcasted_iota(jnp.int32, (m, group), 0)
            ).astype(jnp.float32)
            factor = jnp.dot(cp_ref[...].T, tile_m, precision=lax.Precision.HIGHEST)
            for s in range(ns):
                cps[s * c_all : (s + 1) * c_all] = factor

    @pl.loop(1, nq)
    def _(q):
        for g in range(ng):
            for peer in others_b:
                to_basis(q, g, peer).start()

    gacc[...] = jnp.zeros_like(gacc)

    ch, cl = split2(fc_ref[...])
    dh, dl = split2(bc_ref[...])
    far, relay_half, gram_half = 3 * (me_z - 1), me_z - 1, 2 - me_z

    def relay_group(q, g):
        arrived(far, q, relay_half, g)
        push(far, q, relay_half, g, 3 - me_z)

    def relay(q):
        for g in range(ng):
            relay_group(q, g)

    @pl.loop(0, nq)
    def _(q):
        for g, (at, n, wide) in enumerate(groups):
            block[q, me_b, :, padded[g]] = outgo[me_b, q, :, padded[g]]
            for peer in others_b:
                from_basis(q, g, peer).wait_recv()
            y = left3(ch, cl, block[q, :, :, padded[g]].reshape(c_all, ns * wide))
            y = jnp.concatenate([y[:, s * wide : (s + 1) * wide] for s in range(ns)], axis=0)
            y = right3(y, fh[:wide, :wide], fl[:wide, :wide]) * cps[:, :wide]
            y = right3(y, bh[:wide, :wide], bl[:wide, :wide])
            y = jnp.concatenate([y[s * c_all : (s + 1) * c_all] for s in range(ns)], axis=1)
            y = left3(dh, dl, y)
            if n % LANES:
                full = n - n % LANES
                edge = [y[:, s * wide + full : s * wide + full + LANES] for s in range(ns)]
                wide_low = lax.broadcasted_iota(jnp.int32, edge[0].shape, 1) < LANES // 2
                edge = jnp.where(wide_low, edge[0], pltpu.roll(edge[1], LANES // 2, 1))
                y = jnp.concatenate(
                    [y[:, s * wide : s * wide + full] for s in range(ns)] + [edge], axis=1
                )
            y = y.reshape(rows, 2, lev, ns * n)
            for h in range(2):
                panels[me_z, q, h, :, :, packed[g]] = y[:, h]

            @pl.when(me_z == 0)
            def _():
                push(0, q, 0, g, 1)

                @pl.when(q > 0)
                def _():
                    push(0, q - 1, 1, g, 1)

            @pl.when(me_z == 1)
            def _():
                push(1, q, 0, g, 2)

            @pl.when(me_z == 2)
            def _():
                push(2, q, 1, g, 1)

                @pl.when(q < DIRECT)
                def _():
                    push(2, q, 0, g, 3)

            @pl.when(me_z == 3)
            def _():
                push(3, q, 1, g, 2)

                @pl.when(q > 0)
                def _():
                    push(3, q - 1, 0, g, 2)

            past, back = (1, g + 1) if g < ng - 1 else (0, 0)

            @pl.when(inner & (q >= past) & (q <= past + 1))
            def _():
                relay_group(q - past, back)

    for g in range(ng):
        @pl.when(me_z == 0)
        def _():
            push(0, nq - 1, 1, g, 1)

        @pl.when(me_z == 3)
        def _():
            push(3, nq - 1, 0, g, 2)

    pairs = [(a, b) for a in range(total) for b in range(a + 1)]

    def second(q, g):
        push(1, q, 1, g, 2)
        push(0, q, 1, g, 2)

    def gram_piece(q, h):
        def body(r, accs):
            accs = list(accs)
            for at, n, _ in groups:
                for offs in tiles_of(at, n, ns):
                    vals = []
                    for k in range(nz):
                        vals += load_pair(panels.at[k, q, h, r], low, offs)
                    for p, (a, b) in enumerate(pairs):
                        accs[p] = accs[p] + vals[a] * vals[b]
            return tuple(accs)

        zero = jnp.zeros((lev, LANES), jnp.float32)
        for p, acc in enumerate(lax.fori_loop(0, rows, body, (zero,) * len(pairs))):
            gacc[p] += acc

    row = lax.broadcasted_iota(jnp.int32, (total, LANES), 0)
    col = lax.broadcasted_iota(jnp.int32, (total, LANES), 1)

    @pl.when(inner)
    def _():
        relay(2)

        @pl.loop(0, nq)
        def _(q):
            @pl.when(q == 2)
            def _():
                relay(3)

            @pl.when(q == 3)
            def _():
                relay(4)

                @pl.when(me_z == 1)
                def _():
                    for g in range(AHEAD):
                        second(0, g)

            for g in range(ng):
                arrived(0, q, gram_half, g)
                arrived(3, q, gram_half, g)
                arrived(3 - me_z, q, gram_half, g)

            @pl.when((me_z == 2) & (q < DIRECT))
            def _():
                for g in range(ng):
                    push(1, q, 0, g, 3)
                    push(0, q, 0, g, 3)

            gram_piece(q, gram_half)

        partial = jnp.zeros((total, LANES), jnp.float32)
        for p, (a, b) in enumerate(pairs):
            v = jnp.sum(jnp.sum(gacc[p], axis=0, keepdims=True), axis=1, keepdims=True)
            here = ((row == a) & (col == b)) | ((row == b) & (col == a))
            partial = jnp.where(here, v, partial)
        gram_b[me_b] = partial
        for peer in others_b:
            remote(
                gram_b.at[me_b],
                gram_b.at[me_b],
                gb_send.at[peer],
                gb_recv.at[me_b],
                "basis",
                peer,
            ).start()
        for peer in others_b:
            remote(
                gram_b.at[me_b],
                gram_b.at[peer],
                gb_send.at[peer],
                gb_recv.at[peer],
                "basis",
                peer,
            ).wait()
        partial = gram_b[0]
        for i in range(1, nb):
            partial = partial + gram_b[i]
        gram_z[me_z] = partial
        for peer in others_z:
            remote(
                gram_z.at[me_z],
                gram_z.at[me_z],
                gz_send.at[peer],
                gz_recv.at[me_z],
                "state",
                peer,
            ).start()

        @pl.when(me_z == 1)
        def _():
            for g in range(AHEAD, ng):
                second(0, g)

            @pl.loop(1, nq)
            def _(q):
                for g in range(ng):
                    second(q, g)

    for source in (1, 2):
        @pl.when(me_z != source)
        def _():
            remote(
                gram_z.at[source],
                gram_z.at[source],
                gz_send.at[source],
                gz_recv.at[source],
                "state",
                others_z[0],
            ).wait_recv()

    gram = (gram_z[1] + gram_z[2]) / float(c_all * m * cols)
    pair = jnp.where(col == row + total, 1.0, gram)
    diag = jnp.ones((total, 1), jnp.float32)
    for j in range(total):
        pivot = pair[j : j + 1, j : j + 1]
        diag = jnp.where(row[:, :1] == j, pivot, diag)
        if j < total - 1:
            factor = jnp.where(row[:, :1] > j, pair[:, j : j + 1] / pivot, 0.0)
            pair = pair - factor * pair[j : j + 1, :]
    pair = pair / jnp.sqrt(diag)
    for b in range(total):
        for a in range(b + 1):
            splat[b * total + a] = jnp.broadcast_to(
                pair[b : b + 1, total + a : total + a + 1], (lev, LANES)
            )

    def mix(q, h, g, ins, outs):
        at, n, _ = groups[g]

        @pl.loop(0, rows)
        def _(r):
            for offs in tiles_of(at, n, ns):
                vals = {k: load_pair(panels.at[k, q, h, r], low, offs) for k, _ in ins}
                for panel, dst in outs:
                    res = []
                    for s in range(ns):
                        b = panel * ns + s
                        acc = None
                        for k, ready in ins:
                            if ready:
                                terms = [vals[k][s]]
                            else:
                                terms = [
                                    splat[b * total + k * ns + a] * vals[k][a]
                                    for a in range(ns)
                                    if k * ns + a <= b
                                ]
                            for term in terms:
                                acc = term if acc is None else acc + term
                        res.append(acc)
                    store_pair(dst.at[q, h, r], low, offs, res)

    def plain(*ks):
        return [(k, False) for k in ks]

    def send_home(q, h, g):
        for r in range(rows):
            mine = 2 * r + h == me_b

            @pl.when(jnp.logical_not(mine))
            def _():
                home_out(q, h, g, r).start()

            @pl.when(mine)
            def _():
                home[q, me_b, :, packed[g]] = mixed[q, h, r, :, packed[g]]

    @pl.loop(0, nq)
    def _(q):
        for g in range(ng):
            @pl.when(me_z == 0)
            def _():
                for h in range(2):
                    mix(q, h, g, plain(0), [(0, mixed)])

            @pl.when(me_z == 1)
            def _():
                for h in range(2):
                    mix(q, h, g, plain(0, 1), [(1, mixed)])

            @pl.when(me_z == 2)
            def _():
                mix(q, 0, g, plain(0, 1, 2), [(2, mixed), (3, sums)])

                @pl.when(q >= DIRECT)
                def _():
                    along(sums, 0, q, 0, g, 3).start()

            @pl.when(me_z == 3)
            def _():
                arrived(0, q, 0, g)

                @pl.when(q < DIRECT)
                def _():
                    arrived(1, q, 0, g)
                    arrived(2, q, 0, g)
                    mix(q, 0, g, plain(0, 1, 2, 3), [(3, mixed)])

                @pl.when(q >= DIRECT)
                def _():
                    mix(q, 0, g, [(0, True), (3, False)], [(3, mixed)])

            send_home(q, 0, g)

            @pl.when(me_z <= 1)
            def _():
                send_home(q, 1, g)

    def place(q, g):
        at, n, _ = groups[g]
        full = n - n % LANES
        for peer in others_b:
            home_in(q, g, peer).wait_recv()
        for b in range(nb):
            lane = (b * nq + q) * cols + at
            for s in range(ns):
                src = ns * at + s * full
                o_ref[s, :, lane : lane + full] = home[q, b, :, src : src + full]
                if n % LANES:
                    src = ns * at + ns * full + s * (n - full)
                    o_ref[s, :, lane + full : lane + n] = home[q, b, :, src : src + n - full]

    order = [(q, g) for q in range(nq) for g in range(ng)]
    for k, (q, g) in enumerate(order):
        @pl.when(me_z == 2)
        def _():
            arrived(0, q, 1, g)
            arrived(1, q, 1, g)
            mix(q, 1, g, plain(0, 1, 2), [(2, mixed), (3, sums)])
            along(sums, 0, q, 1, g, 3).start()

        @pl.when(me_z == 3)
        def _():
            arrived(0, q, 1, g)
            mix(q, 1, g, [(0, True), (3, False)], [(3, mixed)])

        @pl.when(me_z >= 2)
        def _():
            send_home(q, 1, g)

        if k >= LAG:
            place(*order[k - LAG])
    for k in range(len(order) - LAG, len(order)):
        place(*order[k])

    @pl.loop(0, nq)
    def _(q):
        for g in range(ng):
            for peer in others_b:
                to_basis(q, g, peer).wait_send()
                home_in(q, g, peer).wait_send()

            @pl.when(me_z == 0)
            def _():
                for h in range(2):
                    sent(0, q, h, g)

            @pl.when(me_z == 1)
            def _():
                for k in range(2):
                    for h in range(2):
                        sent(k, q, h, g)

            @pl.when(me_z == 2)
            def _():
                sent(2, q, 1, g)
                sent(3, q, 1, g)
                sent(0, q, 0, g)
                sent(0, q, 1, g)

                @pl.when(q < DIRECT)
                def _():
                    sent(1, q, 0, g)
                    sent(2, q, 0, g)

            @pl.when(me_z == 3)
            def _():
                for h in range(2):
                    sent(3, q, h, g)

    @pl.when(inner)
    def _():
        for peer in others_z:
            remote(
                gram_z.at[me_z],
                gram_z.at[me_z],
                gz_send.at[peer],
                gz_recv.at[me_z],
                "state",
                peer,
            ).wait_send()


def fast_body(
    nz,
    nb,
    states,
    membrane_step,
    cavity_forward,
    coupling,
    membrane_forward,
    cavity_back,
    membrane_back,
):
    f32, bf16 = jnp.float32, jnp.bfloat16
    ns, lev, joint = states.shape
    m = membrane_step.shape[0]
    c_all = cavity_forward.shape[0]
    nq, rows = m // nb, nb // 2
    cols = joint // m
    group = m * GROUP_BLOCKS
    groups = lane_groups(cols, group)
    ng = len(groups)
    width = sum(wide for _, _, wide in groups)
    total = nz * ns
    dma = pltpu.SemaphoreType.DMA
    vmem = pl.BlockSpec(memory_space=pltpu.VMEM)
    panel = (nq, 2, rows, lev, ns * cols)
    return pl.pallas_call(
        functools.partial(step_kernel, nz, nb),
        in_specs=[pl.BlockSpec(memory_space=pl.ANY)] + [vmem] * 6,
        out_specs=vmem,
        out_shape=jax.ShapeDtypeStruct((ns, lev, joint), f32),
        scratch_shapes=[
            pltpu.VMEM((ns, lev, joint), f32),
            pltpu.VMEM((m * lev, m * lev), bf16),
            pltpu.VMEM((m * lev, m * lev), bf16),
            pltpu.VMEM((m * lev, 3 * m * lev), bf16),
            pltpu.VMEM((m * lev, ns * group), f32),
            pltpu.VMEM((nb, nq, lev, ns * width), f32),
        ]
        + [pltpu.VMEM((group, group), bf16)] * 4
        + [
            pltpu.VMEM((ns * c_all, group), f32),
            pltpu.VMEM((nq, nb, lev, ns * width), f32),
            pltpu.VMEM((nz,) + panel, f32),
            pltpu.VMEM((total * (total + 1) // 2, lev, LANES), f32),
            pltpu.VMEM((nb, total, LANES), f32),
            pltpu.VMEM((nz, total, LANES), f32),
            pltpu.VMEM((total * total, lev, LANES), f32),
            pltpu.VMEM(panel, f32),
            pltpu.VMEM(panel, f32),
            pltpu.VMEM((nq, nb, lev, ns * cols), f32),
            dma((ns, nq)),
        ]
        + [dma((nq, ng, nb))] * 2
        + [dma((nz, nq, 2, ng))] * 2
        + [dma((nb,))] * 2
        + [dma((nz,))] * 2
        + [dma((nq, ng, nb))] * 2,
        compiler_params=pltpu.CompilerParams(
            vmem_limit_bytes=VMEM_LIMIT, collective_id=0, has_side_effects=True
        ),
    )(
        states,
        membrane_step,
        cavity_forward,
        coupling.T,
        membrane_forward,
        cavity_back,
        membrane_back,
    )


def solution(mesh):
    nz, nb = mesh.shape["state"], mesh.shape["basis"]
    in_specs = (P("state", "basis", None), P(), P(), P(), P(), P(), P())
    out_specs = P("state", "basis", None)

    def body(states, membrane_step, cavity_forward, *rest):
        m, c_all = membrane_step.shape[0], cavity_forward.shape[0]
        divides = nz == 4 and m == 5 * nb and nb % 2 == 0
        packs = states.shape[0] == 2 and m * m % LANES == LANES // 2
        if divides and packs and states.shape[1] == 8 and c_all == 8 * nb:
            return fast_body(nz, nb, states, membrane_step, cavity_forward, *rest)
        return plain_body(states, membrane_step, cavity_forward, *rest)

    return jax.shard_map(body, mesh=mesh, in_specs=in_specs, out_specs=out_specs, check_vma=False)
```

```python
import functools

import jax
import jax.numpy as jnp
from jax import lax
from jax.experimental import pallas as pl
from jax.experimental.pallas import tpu as pltpu
from jax.sharding import PartitionSpec as P

LANES = 128
GROUP_BLOCKS = 16
VMEM_LIMIT = 60 * 1024 * 1024
DIRECT = 2
AHEAD = 3
PLACED = 2


def plain_body(
    states, membrane_step, cavity_forward, coupling, membrane_forward, cavity_back, membrane_back
):
    highest = lax.Precision.HIGHEST
    panel_size, level_count, joint = states.shape
    levels_all = cavity_forward.shape[0]
    membrane_levels = membrane_step.shape[0]
    basis_total = float(levels_all * joint)
    head = jnp.einsum(
        "ab,scbr->scar",
        membrane_step,
        states.reshape(panel_size, level_count, membrane_levels, joint // membrane_levels),
        precision=highest,
    )
    head = head.reshape(panel_size, level_count, joint)
    panel_block = lax.all_to_all(head, "basis", split_axis=2, concat_axis=1, tiled=True)
    items, cavity_all, columns = panel_block.shape
    grid = jnp.einsum("qc,kcr->kqr", cavity_forward, panel_block, precision=highest)
    grid = jnp.einsum(
        "kqtm,nm->kqtn",
        grid.reshape(items, cavity_all, columns // membrane_levels, membrane_levels),
        membrane_forward,
        precision=highest,
    )
    weighted = grid * coupling[None, :, None, :]
    backward = jnp.einsum("kqtn,mn->kqtm", weighted, membrane_back, precision=highest)
    backward = backward.reshape(items, cavity_all, columns)
    stepped = jnp.einsum("cq,kqr->kcr", cavity_back, backward, precision=highest)
    spread = lax.all_to_all(stepped, "state", split_axis=2, concat_axis=0, tiled=True)
    state_total, spread_levels, spread_cols = spread.shape
    flattened = spread.reshape(state_total, -1)
    partial_gram = jnp.dot(flattened, flattened.T, precision=highest)
    gram = lax.psum(partial_gram, ("state", "basis")) / basis_total
    lower_factor = jnp.linalg.cholesky(gram)
    identity = jnp.eye(state_total, dtype=gram.dtype)
    inverse = lax.linalg.triangular_solve(lower_factor, identity, left_side=True, lower=True)
    local_result = jnp.dot(inverse, flattened, precision=highest)
    local_result = local_result.reshape(state_total, spread_levels, spread_cols)
    return lax.all_to_all(
        lax.all_to_all(local_result, "state", split_axis=0, concat_axis=2, tiled=True),
        "basis",
        split_axis=1,
        concat_axis=2,
        tiled=True,
    )


def split2(x):
    hi = x.astype(jnp.bfloat16)
    lo = (x - hi.astype(jnp.float32)).astype(jnp.bfloat16)
    return hi, lo


def bdot(a, b):
    return jnp.dot(a, b, preferred_element_type=jnp.float32)


def left3(wh, wl, x):
    xh, xl = split2(x)
    return bdot(jnp.concatenate([wh, wl, wh], axis=1), jnp.concatenate([xh, xh, xl], axis=0))


def right3(x, wh, wl):
    xh, xl = split2(x)
    return bdot(xh, wh) + bdot(xl, wh) + bdot(xh, wl)


def kron_left(w, reps, out_ref_h, out_ref_l):
    m = w.shape[0]
    n = m * reps
    row = lax.broadcasted_iota(jnp.int32, (n, m), 0)
    col = lax.broadcasted_iota(jnp.int32, (n, m), 1)
    left = (row // reps == col).astype(jnp.bfloat16)
    right_row = lax.broadcasted_iota(jnp.int32, (m, n), 0)
    right_col = lax.broadcasted_iota(jnp.int32, (m, n), 1)
    right = (right_col // reps == right_row).astype(jnp.bfloat16)
    a = lax.broadcasted_iota(jnp.int32, (n, 1), 0)
    b = lax.broadcasted_iota(jnp.int32, (1, n), 1)
    keep = lax.rem(a, reps) == lax.rem(b, reps)
    for part, ref in zip(split2(w), (out_ref_h, out_ref_l)):
        full = bdot(bdot(left, part).astype(jnp.bfloat16), right)
        ref[...] = jnp.where(keep, full, 0.0).astype(jnp.bfloat16)


def kron_lanes(w_t, reps, out_ref_h, out_ref_l):
    m = w_t.shape[0]
    n = m * reps
    left = (
        lax.rem(lax.broadcasted_iota(jnp.int32, (n, m), 0), m)
        == lax.broadcasted_iota(jnp.int32, (n, m), 1)
    ).astype(jnp.bfloat16)
    right = (
        lax.rem(lax.broadcasted_iota(jnp.int32, (m, n), 1), m)
        == lax.broadcasted_iota(jnp.int32, (m, n), 0)
    ).astype(jnp.bfloat16)
    a = lax.broadcasted_iota(jnp.int32, (n, 1), 0)
    b = lax.broadcasted_iota(jnp.int32, (1, n), 1)
    keep = a // m == b // m
    for part, ref in zip(split2(w_t), (out_ref_h, out_ref_l)):
        full = bdot(bdot(left, part).astype(jnp.bfloat16), right)
        ref[...] = jnp.where(keep, full, 0.0).astype(jnp.bfloat16)


def remote(src, dst, send_sem, recv_sem, axis, peer):
    return pltpu.make_async_remote_copy(
        src_ref=src,
        dst_ref=dst,
        send_sem=send_sem,
        recv_sem=recv_sem,
        device_id={axis: peer},
        device_id_type=pl.DeviceIdType.MESH,
    )


def peers_of(axis, size):
    me = lax.axis_index(axis)
    return me, [lax.rem(me + d, size) for d in range(1, size)]


def lane_groups(cols, group):
    out = []
    for at in range(0, cols, group):
        n = min(group, cols - at)
        out.append((at, n, -(-n // LANES) * LANES))
    return out


def tiles_of(at, n, ns):
    for t in range(n // LANES):
        yield [ns * at + s * (n // LANES) * LANES + t * LANES for s in range(ns)]
    if n % LANES:
        yield [ns * at + ns * (n // LANES) * LANES]


def load_pair(ref, low, offs):
    vals = [ref[:, at : at + LANES] for at in offs]
    if len(vals) == 1:
        v = vals[0]
        vals = [jnp.where(low, v, 0.0), jnp.where(low, pltpu.roll(v, LANES // 2, 1), 0.0)]
    return vals


def store_pair(ref, low, offs, vals):
    if len(offs) == 1:
        vals = [jnp.where(low, vals[0], pltpu.roll(vals[1], LANES // 2, 1))]
    for at, v in zip(offs, vals):
        ref[:, at : at + LANES] = v


def step_kernel(
    nz,
    nb,
    x_ref,
    ms_ref,
    fc_ref,
    cp_ref,
    fk_ref,
    bc_ref,
    bk_ref,
    home,
    xin,
    kh,
    kl,
    kcat,
    xs,
    outgo,
    fh,
    fl,
    bh,
    bl,
    cps,
    block,
    panels,
    gacc,
    gram_b,
    gram_z,
    splat,
    mixed,
    sums,
    in_sem,
    b_send,
    b_recv,
    z_send,
    z_recv,
    gb_send,
    gb_recv,
    gz_send,
    gz_recv,
    c_send,
    c_recv,
):
    ns, lev, _ = xin.shape
    nq = block.shape[0]
    rows = nb // 2
    total = nz * ns
    c_all = fc_ref.shape[0]
    m = fk_ref.shape[0]
    cols = x_ref.shape[2] // m
    group = m * GROUP_BLOCKS
    groups = lane_groups(cols, group)
    ng = len(groups)
    padded = [pl.ds(ns * at, ns * wide) for at, _, wide in groups]
    packed = [pl.ds(ns * at, ns * n) for at, n, _ in groups]
    me_b, others_b = peers_of("basis", nb)
    me_z, others_z = peers_of("state", nz)
    parity = lax.rem(me_b, 2)
    inner = (me_z == 1) | (me_z == 2)
    low = lax.broadcasted_iota(jnp.int32, (lev, LANES), 1) < LANES // 2

    def to_basis(q, g, peer):
        return remote(
            outgo.at[peer, q, :, padded[g]],
            block.at[q, me_b, :, padded[g]],
            b_send.at[q, g, peer],
            b_recv.at[q, g, me_b],
            "basis",
            peer,
        )

    def from_basis(q, g, peer):
        return remote(
            outgo.at[me_b, q, :, padded[g]],
            block.at[q, peer, :, padded[g]],
            b_send.at[q, g, peer],
            b_recv.at[q, g, peer],
            "basis",
            peer,
        )

    def along(src, slot, q, h, g, peer):
        return remote(
            src.at[q, h, :, :, packed[g]],
            panels.at[slot, q, h, :, :, packed[g]],
            z_send.at[slot, q, h, g],
            z_recv.at[slot, q, h, g],
            "state",
            peer,
        )

    def push(k, q, h, g, peer):
        along(panels.at[k], k, q, h, g, peer).start()

    def arrived(slot, q, h, g):
        along(mixed, slot, q, h, g, others_z[0]).wait_recv()

    def sent(slot, q, h, g):
        along(mixed, slot, q, h, g, others_z[0]).wait_send()

    def home_out(q, h, g, r):
        peer = 2 * r + h
        return remote(
            mixed.at[q, h, r, :, packed[g]],
            home.at[q, me_b, :, packed[g]],
            c_send.at[q, g, peer],
            c_recv.at[q, g, me_b],
            "basis",
            peer,
        )

    def keep(q, h, g, r):
        return pltpu.make_async_copy(
            mixed.at[q, h, r, :, packed[g]],
            home.at[q, me_b, :, packed[g]],
            c_send.at[q, g, me_b],
        )

    def home_in(q, g, peer):
        return remote(
            mixed.at[q, 0, 0, :, packed[g]],
            home.at[q, peer, :, packed[g]],
            c_send.at[q, g, peer],
            c_recv.at[q, g, peer],
            "basis",
            peer,
        )

    barrier = pltpu.get_barrier_semaphore()
    for axis, others in (("basis", others_b), ("state", others_z)):
        for peer in others:
            pl.semaphore_signal(
                barrier, inc=1, device_id={axis: peer}, device_id_type=pl.DeviceIdType.MESH
            )
    def load(s, c):
        lanes = pl.ds(c * nb * cols, nb * cols)
        return pltpu.make_async_copy(x_ref.at[s, :, lanes], xin.at[s, :, lanes], in_sem.at[s, c])

    for c in range(m // nb):
        for s in range(ns):
            load(s, c).start()
    kron_left(ms_ref[...], lev, kh, kl)
    kcat[...] = jnp.concatenate([kh[...], kl[...], kh[...]], axis=1)
    for g, (at, n, wide) in enumerate(groups):
        for i in range(m):
            for s in range(ns):
                if g == 0 and i % nb == 0:
                    load(s, i // nb).wait()
                xs[i * lev : (i + 1) * lev, s * wide : s * wide + n] = xin[
                    s, :, i * cols + at : i * cols + at + n
                ]
        xh, xl = split2(xs[:, : ns * wide])
        y = bdot(kcat[...], jnp.concatenate([xh, xh, xl], axis=0))
        outgo[:, :, :, padded[g]] = y.reshape(nb, nq, lev, ns * wide)
        if g == 0:
            pl.semaphore_wait(barrier, nb + nz - 2)
        for peer in others_b:
            to_basis(0, g, peer).start()
        if g == 0:
            kron_lanes(fk_ref[...].T, GROUP_BLOCKS, fh, fl)
            kron_lanes(bk_ref[...].T, GROUP_BLOCKS, bh, bl)
            tile_m = (
                lax.rem(lax.broadcasted_iota(jnp.int32, (m, group), 1), m)
                == lax.broadcasted_iota(jnp.int32, (m, group), 0)
            ).astype(jnp.float32)
            factor = jnp.dot(cp_ref[...].T, tile_m, precision=lax.Precision.HIGHEST)
            for s in range(ns):
                cps[s * c_all : (s + 1) * c_all] = factor

    @pl.loop(1, nq)
    def _(q):
        for g in range(ng):
            for peer in others_b:
                to_basis(q, g, peer).start()

    gacc[...] = jnp.zeros_like(gacc)

    ch, cl = split2(fc_ref[...])
    dh, dl = split2(bc_ref[...])
    far, relay_half, gram_half = 3 * (me_z - 1), me_z - 1, 2 - me_z

    def relay_group(q, g):
        arrived(far, q, relay_half, g)
        push(far, q, relay_half, g, 3 - me_z)

    def relay(q):
        for g in range(ng):
            relay_group(q, g)

    @pl.loop(0, nq)
    def _(q):
        for g, (at, n, wide) in enumerate(groups):
            block[q, me_b, :, padded[g]] = outgo[me_b, q, :, padded[g]]
            for peer in others_b:
                from_basis(q, g, peer).wait_recv()
            y = left3(ch, cl, block[q, :, :, padded[g]].reshape(c_all, ns * wide))
            y = jnp.concatenate([y[:, s * wide : (s + 1) * wide] for s in range(ns)], axis=0)
            y = right3(y, fh[:wide, :wide], fl[:wide, :wide]) * cps[:, :wide]
            y = right3(y, bh[:wide, :wide], bl[:wide, :wide])
            y = jnp.concatenate([y[s * c_all : (s + 1) * c_all] for s in range(ns)], axis=1)
            y = left3(dh, dl, y)
            if n % LANES:
                full = n - n % LANES
                edge = [y[:, s * wide + full : s * wide + full + LANES] for s in range(ns)]
                wide_low = lax.broadcasted_iota(jnp.int32, edge[0].shape, 1) < LANES // 2
                edge = jnp.where(wide_low, edge[0], pltpu.roll(edge[1], LANES // 2, 1))
                y = jnp.concatenate(
                    [y[:, s * wide : s * wide + full] for s in range(ns)] + [edge], axis=1
                )
            y = y.reshape(rows, 2, lev, ns * n)
            for h in range(2):
                panels[me_z, q, h, :, :, packed[g]] = y[:, h]

            @pl.when(me_z == 0)
            def _():
                push(0, q, 0, g, 1)

                @pl.when(q > 0)
                def _():
                    push(0, q - 1, 1, g, 1)

            @pl.when(me_z == 1)
            def _():
                push(1, q, 0, g, 2)

            @pl.when(me_z == 2)
            def _():
                push(2, q, 1, g, 1)

                @pl.when(q < DIRECT)
                def _():
                    push(2, q, 0, g, 3)

            @pl.when(me_z == 3)
            def _():
                push(3, q, 1, g, 2)

                @pl.when(q > 0)
                def _():
                    push(3, q - 1, 0, g, 2)

            past, back = (1, g + 1) if g < ng - 1 else (0, 0)

            @pl.when(inner & (q >= past) & (q <= past + 1))
            def _():
                relay_group(q - past, back)

    for g in range(ng):
        @pl.when(me_z == 0)
        def _():
            push(0, nq - 1, 1, g, 1)

        @pl.when(me_z == 3)
        def _():
            push(3, nq - 1, 0, g, 2)

    pairs = [(a, b) for a in range(total) for b in range(a + 1)]

    def second(q, g):
        push(1, q, 1, g, 2)
        push(0, q, 1, g, 2)

    def gram_piece(q, h):
        def body(r, accs):
            accs = list(accs)
            for at, n, _ in groups:
                for offs in tiles_of(at, n, ns):
                    vals = []
                    for k in range(nz):
                        vals += load_pair(panels.at[k, q, h, r], low, offs)
                    for p, (a, b) in enumerate(pairs):
                        accs[p] = accs[p] + vals[a] * vals[b]
            return tuple(accs)

        zero = jnp.zeros((lev, LANES), jnp.float32)
        for p, acc in enumerate(lax.fori_loop(0, rows, body, (zero,) * len(pairs))):
            gacc[p] += acc

    row = lax.broadcasted_iota(jnp.int32, (total, LANES), 0)
    col = lax.broadcasted_iota(jnp.int32, (total, LANES), 1)

    @pl.when(inner)
    def _():
        relay(2)

        @pl.loop(0, nq)
        def _(q):
            @pl.when(q == 2)
            def _():
                relay(3)

            @pl.when(q == 3)
            def _():
                relay(4)

                @pl.when(me_z == 1)
                def _():
                    for g in range(AHEAD):
                        second(0, g)

            for g in range(ng):
                arrived(0, q, gram_half, g)
                arrived(3, q, gram_half, g)
                arrived(3 - me_z, q, gram_half, g)

            @pl.when((me_z == 2) & (q < DIRECT))
            def _():
                for g in range(ng):
                    push(1, q, 0, g, 3)
                    push(0, q, 0, g, 3)

            gram_piece(q, gram_half)

        partial = jnp.zeros((total, LANES), jnp.float32)
        for p, (a, b) in enumerate(pairs):
            v = jnp.sum(jnp.sum(gacc[p], axis=0, keepdims=True), axis=1, keepdims=True)
            here = ((row == a) & (col == b)) | ((row == b) & (col == a))
            partial = jnp.where(here, v, partial)
        gram_b[me_b] = partial
        for peer in others_b:
            remote(
                gram_b.at[me_b],
                gram_b.at[me_b],
                gb_send.at[peer],
                gb_recv.at[me_b],
                "basis",
                peer,
            ).start()
        for peer in others_b:
            remote(
                gram_b.at[me_b],
                gram_b.at[peer],
                gb_send.at[peer],
                gb_recv.at[peer],
                "basis",
                peer,
            ).wait()
        partial = gram_b[0]
        for i in range(1, nb):
            partial = partial + gram_b[i]
        gram_z[me_z] = partial
        for peer in others_z:
            remote(
                gram_z.at[me_z],
                gram_z.at[me_z],
                gz_send.at[peer],
                gz_recv.at[me_z],
                "state",
                peer,
            ).start()

        @pl.when(me_z == 1)
        def _():
            for g in range(AHEAD, ng):
                second(0, g)

            @pl.loop(1, nq)
            def _(q):
                for g in range(ng):
                    second(q, g)

    for source in (1, 2):
        @pl.when(me_z != source)
        def _():
            remote(
                gram_z.at[source],
                gram_z.at[source],
                gz_send.at[source],
                gz_recv.at[source],
                "state",
                others_z[0],
            ).wait_recv()

    gram = (gram_z[1] + gram_z[2]) / float(c_all * m * cols)
    pair = jnp.where(col == row + total, 1.0, gram)
    diag = jnp.ones((total, 1), jnp.float32)
    for j in range(total):
        pivot = pair[j : j + 1, j : j + 1]
        diag = jnp.where(row[:, :1] == j, pivot, diag)
        if j < total - 1:
            factor = jnp.where(row[:, :1] > j, pair[:, j : j + 1] / pivot, 0.0)
            pair = pair - factor * pair[j : j + 1, :]
    pair = pair / jnp.sqrt(diag)
    for b in range(total):
        for a in range(b + 1):
            splat[b * total + a] = jnp.broadcast_to(
                pair[b : b + 1, total + a : total + a + 1], (lev, LANES)
            )

    def mix(q, h, g, ins, outs):
        at, n, _ = groups[g]

        @pl.loop(0, rows)
        def _(r):
            for offs in tiles_of(at, n, ns):
                vals = {k: load_pair(panels.at[k, q, h, r], low, offs) for k, _ in ins}
                for panel, dst in outs:
                    res = []
                    for s in range(ns):
                        b = panel * ns + s
                        acc = None
                        for k, ready in ins:
                            if ready:
                                terms = [vals[k][s]]
                            else:
                                terms = [
                                    splat[b * total + k * ns + a] * vals[k][a]
                                    for a in range(ns)
                                    if k * ns + a <= b
                                ]
                            for term in terms:
                                acc = term if acc is None else acc + term
                        res.append(acc)
                    store_pair(dst.at[q, h, r], low, offs, res)

    def plain(*ks):
        return [(k, False) for k in ks]

    def send_home(q, h, g):
        for r in range(rows):
            mine = 2 * r + h == me_b

            @pl.when(jnp.logical_not(mine))
            def _():
                home_out(q, h, g, r).start()

            @pl.when(mine)
            def _():
                keep(q, h, g, r).start()

    @pl.loop(0, nq)
    def _(q):
        for g in range(ng):
            @pl.when(me_z == 0)
            def _():
                for h in range(2):
                    mix(q, h, g, plain(0), [(0, mixed)])

            @pl.when(me_z == 1)
            def _():
                for h in range(2):
                    mix(q, h, g, plain(0, 1), [(1, mixed)])

            @pl.when(me_z == 2)
            def _():
                mix(q, 0, g, plain(0, 1, 2), [(2, mixed), (3, sums)])

                @pl.when(q >= DIRECT)
                def _():
                    along(sums, 0, q, 0, g, 3).start()

            @pl.when(me_z == 3)
            def _():
                arrived(0, q, 0, g)

                @pl.when(q < DIRECT)
                def _():
                    arrived(1, q, 0, g)
                    arrived(2, q, 0, g)
                    mix(q, 0, g, plain(0, 1, 2, 3), [(3, mixed)])

                @pl.when(q >= DIRECT)
                def _():
                    mix(q, 0, g, [(0, True), (3, False)], [(3, mixed)])

            send_home(q, 0, g)

            @pl.when(me_z <= 1)
            def _():
                send_home(q, 1, g)

    @pl.loop(0, nq)
    def _(q):
        for g in range(ng):
            @pl.when(me_z == 2)
            def _():
                arrived(0, q, 1, g)
                arrived(1, q, 1, g)
                mix(q, 1, g, plain(0, 1, 2), [(2, mixed), (3, sums)])
                along(sums, 0, q, 1, g, 3).start()

            @pl.when(me_z == 3)
            def _():
                arrived(0, q, 1, g)
                mix(q, 1, g, [(0, True), (3, False)], [(3, mixed)])

            @pl.when(me_z >= 2)
            def _():
                send_home(q, 1, g)

    @pl.loop(0, nq)
    def _(q):
        for g in range(ng):
            for peer in others_b:
                to_basis(q, g, peer).wait_send()
                home_in(q, g, peer).wait()
            keep(q, 0, g, 0).wait()

            @pl.when(me_z == 0)
            def _():
                for h in range(2):
                    sent(0, q, h, g)

            @pl.when(me_z == 1)
            def _():
                for k in range(2):
                    for h in range(2):
                        sent(k, q, h, g)

            @pl.when(me_z == 2)
            def _():
                sent(2, q, 1, g)
                sent(3, q, 1, g)
                sent(0, q, 0, g)
                sent(0, q, 1, g)

                @pl.when(q < DIRECT)
                def _():
                    sent(1, q, 0, g)
                    sent(2, q, 0, g)

            @pl.when(me_z == 3)
            def _():
                for h in range(2):
                    sent(3, q, h, g)

    @pl.when(inner)
    def _():
        for peer in others_z:
            remote(
                gram_z.at[me_z],
                gram_z.at[me_z],
                gz_send.at[peer],
                gz_recv.at[me_z],
                "state",
                peer,
            ).wait_send()


def place_kernel(group, home, o_ref):
    nq, pair, _, packed = home.shape
    ns = o_ref.shape[0]
    cols = packed // ns
    for b in range(pair):
        for q in range(nq):
            lane = (b * nq + q) * cols
            for at, n, _ in lane_groups(cols, group):
                full = n - n % LANES
                for s in range(ns):
                    src = ns * at + s * full
                    to = lane + at
                    o_ref[s, :, to : to + full] = home[q, b, :, src : src + full]
                    if n % LANES:
                        src = ns * (at + full) + s * (n - full)
                        o_ref[s, :, to + full : to + n] = home[q, b, :, src : src + n - full]


def fast_body(
    nz,
    nb,
    states,
    membrane_step,
    cavity_forward,
    coupling,
    membrane_forward,
    cavity_back,
    membrane_back,
):
    f32, bf16 = jnp.float32, jnp.bfloat16
    ns, lev, joint = states.shape
    m = membrane_step.shape[0]
    c_all = cavity_forward.shape[0]
    nq, rows = m // nb, nb // 2
    cols = joint // m
    group = m * GROUP_BLOCKS
    groups = lane_groups(cols, group)
    ng = len(groups)
    width = sum(wide for _, _, wide in groups)
    total = nz * ns
    dma = pltpu.SemaphoreType.DMA
    vmem = pl.BlockSpec(memory_space=pltpu.VMEM)
    panel = (nq, 2, rows, lev, ns * cols)
    home = pl.pallas_call(
        functools.partial(step_kernel, nz, nb),
        in_specs=[pl.BlockSpec(memory_space=pl.ANY)] + [vmem] * 6,
        out_specs=pl.BlockSpec(memory_space=pl.ANY),
        out_shape=jax.ShapeDtypeStruct((nq, nb, lev, ns * cols), f32),
        scratch_shapes=[
            pltpu.VMEM((ns, lev, joint), f32),
            pltpu.VMEM((m * lev, m * lev), bf16),
            pltpu.VMEM((m * lev, m * lev), bf16),
            pltpu.VMEM((m * lev, 3 * m * lev), bf16),
            pltpu.VMEM((m * lev, ns * group), f32),
            pltpu.VMEM((nb, nq, lev, ns * width), f32),
        ]
        + [pltpu.VMEM((group, group), bf16)] * 4
        + [
            pltpu.VMEM((ns * c_all, group), f32),
            pltpu.VMEM((nq, nb, lev, ns * width), f32),
            pltpu.VMEM((nz,) + panel, f32),
            pltpu.VMEM((total * (total + 1) // 2, lev, LANES), f32),
            pltpu.VMEM((nb, total, LANES), f32),
            pltpu.VMEM((nz, total, LANES), f32),
            pltpu.VMEM((total * total, lev, LANES), f32),
            pltpu.VMEM(panel, f32),
            pltpu.VMEM(panel, f32),
            dma((ns, nq)),
        ]
        + [dma((nq, ng, nb))] * 2
        + [dma((nz, nq, 2, ng))] * 2
        + [dma((nb,))] * 2
        + [dma((nz,))] * 2
        + [dma((nq, ng, nb))] * 2,
        compiler_params=pltpu.CompilerParams(
            vmem_limit_bytes=VMEM_LIMIT, collective_id=0, has_side_effects=True
        ),
    )(
        states,
        membrane_step,
        cavity_forward,
        coupling.T,
        membrane_forward,
        cavity_back,
        membrane_back,
    )
    return pl.pallas_call(
        functools.partial(place_kernel, group),
        grid=(nb // PLACED,),
        in_specs=[pl.BlockSpec((nq, PLACED, lev, ns * cols), lambda i: (0, i, 0, 0))],
        out_specs=pl.BlockSpec((ns, lev, PLACED * nq * cols), lambda i: (0, 0, i)),
        out_shape=jax.ShapeDtypeStruct((ns, lev, joint), f32),
    )(home)


def solution(mesh):
    nz, nb = mesh.shape["state"], mesh.shape["basis"]
    in_specs = (P("state", "basis", None), P(), P(), P(), P(), P(), P())
    out_specs = P("state", "basis", None)

    def body(states, membrane_step, cavity_forward, *rest):
        m, c_all = membrane_step.shape[0], cavity_forward.shape[0]
        divides = nz == 4 and m == 5 * nb and nb % 2 == 0
        packs = states.shape[0] == 2 and m * m % LANES == LANES // 2
        if divides and packs and states.shape[1] == 8 and c_all == 8 * nb:
            return fast_body(nz, nb, states, membrane_step, cavity_forward, *rest)
        return plain_body(states, membrane_step, cavity_forward, *rest)

    return jax.shard_map(body, mesh=mesh, in_specs=in_specs, out_specs=out_specs, check_vma=False)
```
